32 devices in a mesh: rcv: 4 (over y, core), slab: 8 (over z, x).
Axes of the slice: x: 2, y: 2, z: 4, core: 2. Of those that a mesh axis runs over, the one named last changes fastest.
Arguments:
- displacement: bfloat16 [2, 16, 3, 16, 16, 1024], P(None, None, None, 'slab'), may hold values from -6 to 6
- green: bfloat16 [8, 16, 6, 16, 16, 1024], P('rcv', None, None, 'slab'), may hold values from -0.1796875 to 0.1796875
- lame_lambda: float32 [16, 16, 1024], P('slab'), may hold values from 0.5 to 2
- shear_modulus: float32 [16, 16, 1024], P('slab'), may hold values from 0.3 to 1.5
- filters: float32 [2, 8, 9], P(None, 'rcv'), may hold values from -2 to 2
- pairs: int32 [2, 8], P(None, 'rcv'), may hold values 0 or 1
Outputs:
- kernels: float32 [2, 16, 16, 1024], P(None, 'slab', 'rcv')
The draws below stay inside these ranges and needn't reach their ends.
Inputs may be any that keep to these rules, and one draw needn't show every extreme that they name: `pairs`: 1 marks a pair that is used, 0 one that is not.
All inputs are finite; a program needn't handle non-finite values. No bound on the sum of `pairs` on one device may be relied on, other than what follows from the above.
Results may differ from the reference program's by a relative error of at most 0.0029.
Values may be sent and summed in bfloat16 or wider, within the bound.
No kernel may reach another device: no remote copies, remote signals or barrier semaphores. Data moves between devices by JAX's collectives and lax.ppermute only.
A program may use at most 192 MiB of HBM per device.

```python
import math
import jax
import jax.numpy as jnp
from jax import lax

E = 2
SNAP = 16
LAGS = 9
ROWS = 16
COLS = 1024
NZ = 16
RECEIVERS = 8


def with_ends(values, rng, least, high):
    shape = values.shape
    spot = [jax.random.randint(jax.random.fold_in(rng, axis), (), 0, shape[axis]) for axis in range(len(shape))]
    values = values.at[tuple(spot)].set(least)
    longest = shape.index(max(shape))
    spot[longest] = (spot[longest] + 1) % shape[longest]
    return values.at[tuple(spot)].set(high)


def raised(values, own_key, source, target, shards_of, factor):
    def block_of(axis_at):
        return (jnp.arange(values.shape[axis_at]) // (values.shape[axis_at] // shards_of)).reshape((-1,) + (1,) * (values.ndim - 1 - axis_at))

    first = jax.random.permutation(own_key, shards_of)[block_of(target)]
    second = (block_of(target) + shards_of // 2) % shards_of
    return jnp.where((block_of(source) == first) | (block_of(source) == second), factor * values, values)


def steps_of(rng, shape, pieces, smallest, top_value):
    loudness, own = 1.0, jax.random.fold_in(rng, 6)
    for dim, blocks in pieces:
        heights = jnp.exp(jax.random.uniform(jax.random.fold_in(own, dim), (blocks,), jnp.float32, smallest / len(pieces), top_value / len(pieces)))
        loudness = loudness * jnp.repeat(heights, shape[dim] // blocks).reshape([-1 if axis == dim else 1 for axis in range(len(shape))])
    return loudness


def scatter_about(key, dims, deviation, most, split=(), dtype=jnp.bfloat16):
    entries = deviation * jax.random.normal(key, dims, jnp.float32)
    if split:
        entries = entries * steps_of(key, dims, split, -0.22, 0.18)
    return jnp.clip(entries, -most, most).astype(dtype)


def heavy_noise(key, dims, scale, limit, cuts, heavy, dtype=jnp.bfloat16):
    values = scale * jax.random.normal(key, dims, jnp.float32)
    if cuts:
        values = values * steps_of(key, dims, cuts, -0.22, 0.18)
    return jnp.clip(raised(values, jax.random.fold_in(key, 3), *heavy), -limit, limit).astype(dtype)


def setup_inputs(seed: int = 0) -> dict:
    key_of = jax.random.split(jax.random.key(seed), 7)
    return {
        "displacement": scatter_about(key_of[0], (E, SNAP, 3, NZ, ROWS, COLS), 1.0, 6.0, ((3, 8),)),
        "green": heavy_noise(key_of[1], (RECEIVERS, SNAP, 6, NZ, ROWS, COLS), 0.03, 0.1796875, ((0, 4), (3, 8)), (0, 4, 4, 2.0)),
        "lame_lambda": jnp.clip(jnp.exp(math.log(2.0) - 1.3862944 * jax.random.uniform(key_of[2], (NZ, ROWS, COLS), jnp.float32) ** steps_of(key_of[2], (NZ, ROWS, COLS), ((0, 8),), -0.2, 0.2)), 0.5, 2.0),
        "shear_modulus": jnp.clip(jnp.exp(math.log(1.5) - 1.60943787 * jax.random.uniform(key_of[3], (NZ, ROWS, COLS), jnp.float32) ** steps_of(key_of[3], (NZ, ROWS, COLS), ((0, 8),), -0.2, 0.2)), 0.3, 1.5),
        "filters": scatter_about(key_of[4], (E, RECEIVERS, LAGS), 0.35, 2.0, ((1, 4),), jnp.float32),
        "pairs": with_ends((jax.random.randint(key_of[5], (E, RECEIVERS), 0, 2) < 1).astype(jnp.int32), jax.random.fold_in(key_of[5], 1), 0, 1),
    }


def derivative(field, axis):
    length = field.shape[axis]
    pad_width = [(0, 0)] * field.ndim
    pad_width[axis] = (2, 2)
    padded = jnp.pad(field, pad_width)

    def window(offset):
        return lax.slice_in_dim(padded, 2 + offset, 2 + offset + length, axis=axis)

    return (8.0 * (window(1) - window(-1)) - (window(2) - window(-2))) / 12.0


def compose(along_cols, along_rows, along_depth, lame_lambda, shear_modulus):
    strain_xx = along_cols[:, :, 0]
    strain_yy = along_rows[:, :, 1]
    strain_zz = along_depth[:, :, 2]
    strain_yz = 0.5 * (along_depth[:, :, 1] + along_rows[:, :, 2])
    strain_xz = 0.5 * (along_depth[:, :, 0] + along_cols[:, :, 2])
    strain_xy = 0.5 * (along_rows[:, :, 0] + along_cols[:, :, 1])
    strain_trace = strain_xx + strain_yy + strain_zz
    volume_term = lame_lambda * strain_trace
    double_shear = 2.0 * shear_modulus
    components = [volume_term + double_shear * strain_xx, volume_term + double_shear * strain_yy,
                  volume_term + double_shear * strain_zz, double_shear * strain_yz,
                  double_shear * strain_xz, double_shear * strain_xy]
    return jnp.stack(components, axis=2).astype(jnp.bfloat16)


def contribution(stress_one, filter_taps, green_one):
    lag_total = filter_taps.shape[0]
    half_lags = lag_total // 2
    snap_count = stress_one.shape[0]
    padded = jnp.pad(stress_one, [(half_lags, half_lags)] + [(0, 0)] * (stress_one.ndim - 1))
    filtered = jnp.zeros(stress_one.shape, jnp.float32)
    for lag_index in range(lag_total):
        filtered = filtered + filter_taps[lag_index] * padded[lag_index:lag_index + snap_count].astype(jnp.float32)
    weights = jnp.array([1.0, 1.0, 1.0, 2.0, 2.0, 2.0], jnp.float32).reshape(1, 6, 1, 1, 1)
    return jnp.sum(filtered * green_one.astype(jnp.float32) * weights, axis=(0, 1))


def reference(displacement, green, lame_lambda, shear_modulus, filters, pairs):
    field = displacement.astype(jnp.float32)
    along_cols = derivative(field, 5)
    along_rows = derivative(field, 4)
    along_depth = derivative(field, 3)
    stress = compose(along_cols, along_rows, along_depth, lame_lambda, shear_modulus)
    initial = jnp.zeros((E, NZ, ROWS, COLS), jnp.float32)

    def receiver_step(kernel_total, scanned):
        green_one, filter_rows, pair_row = scanned
        per_source = [pair_row[source].astype(jnp.float32) * contribution(stress[source], filter_rows[source], green_one)
                      for source in range(E)]
        return kernel_total + jnp.stack(per_source), None

    kernel_total, unused = lax.scan(receiver_step, initial,
                                    (green, jnp.swapaxes(filters, 0, 1), jnp.swapaxes(pairs, 0, 1)))
    return kernel_total
```

```python
import functools
import jax
import jax.numpy as jnp
from jax import lax
from jax.experimental import pallas as pl
from jax.experimental.pallas import tpu as pltpu
from jax.sharding import PartitionSpec as P

LANES = 128
F32 = jnp.float32
BF16 = jnp.bfloat16
ANY = pl.BlockSpec(memory_space=pl.ANY)
SMEM = pl.BlockSpec(memory_space=pltpu.SMEM)
VMEM = pl.BlockSpec(memory_space=pltpu.VMEM)


def stencil(offset):
    return (
        jnp.where(offset == 1, 8.0, 0.0)
        + jnp.where(offset == -1, -8.0, 0.0)
        + jnp.where(offset == 2, -1.0, 0.0)
        + jnp.where(offset == -2, 1.0, 0.0)
    )


def iota(shape, axis):
    return lax.broadcasted_iota(jnp.int32, shape, axis)


def mm(a, b):
    return jnp.dot(a, b, preferred_element_type=F32)


def fill_tables(filters_ref, pairs_ref, mix_ref, dcol_ref, drow_ref, rows):
    sources, stations, lags = filters_ref.shape
    points = mix_ref.shape[0] // sources
    snaps = points // rows
    depth = mix_ref.shape[1]
    shape = (snaps, stations * snaps)
    station, at = iota(shape, 1) // snaps, iota(shape, 1) % snaps
    lag = iota(shape, 0) - at + lags // 2
    spread = (iota((points, snaps), 0) // rows == iota((points, snaps), 1)).astype(BF16)
    fan = (iota((depth // rows, depth), 1) // rows == iota((depth // rows, depth), 0)).astype(BF16)
    same = iota((points, depth), 0) % rows == iota((points, depth), 1) % rows
    for e in range(sources):
        table = jnp.zeros(shape, F32)
        for r in range(stations):
            used = pairs_ref[e, r].astype(F32)
            for j in range(lags):
                table = jnp.where((station == r) & (lag == j), used * filters_ref[e, r, j], table)
        high = table.astype(BF16)
        low = (table - high.astype(F32)).astype(BF16)
        taps = jnp.concatenate([high, low], axis=1)
        full = mm(mm(spread, taps).astype(BF16), fan)
        mix_ref[pl.ds(e * points, points)] = jnp.where(same, full, 0.0).astype(BF16)
    shape = dcol_ref.shape
    width = shape[1]
    place = iota(shape, 0)
    source = jnp.where(place < width, place, jnp.where(place < width + LANES, place - width - LANES, place - LANES))
    dcol_ref[...] = stencil(source - iota(shape, 1)).astype(BF16)
    shape = drow_ref.shape[1:]
    row, full = iota(shape, 0), iota(shape, 1)
    near = row // rows == full // (2 * rows)
    for h in range(2):
        drow_ref[h] = jnp.where(near, stencil(full % (2 * rows) - row % rows - h * rows), 0.0).astype(BF16)


def prepare(array, block, width, sizes, filters, pairs, snaps):
    tail = array.shape[1:-1] + (width,)
    starts = [sum(sizes[:k]) for k in range(len(sizes))]
    sources, stations, _ = filters.shape
    rows = array.shape[-2]
    points = snaps * rows // 2
    pieces = len(sizes)

    def kernel(block_ref, filters_ref, pairs_ref, src, *rest):
        outs, (mix_ref, dcol_ref, drow_ref, held, sems) = rest[:pieces], rest[pieces:]
        start = pl.multiple_of(block_ref[0] * width, width)
        spans = [pl.ds(at, size) for at, size in zip(starts, sizes)]
        gets = [
            pltpu.make_async_copy(src.at[span, ..., pl.ds(start, width)], held.at[span], sems.at[0, k])
            for k, span in enumerate(spans)
        ]
        puts = [pltpu.make_async_copy(held.at[span], outs[k], sems.at[1, k]) for k, span in enumerate(spans)]
        for get in gets:
            get.start()
        fill_tables(filters_ref, pairs_ref, mix_ref, dcol_ref, drow_ref, rows // 2)
        for get, put in zip(gets, puts):
            get.wait()
            put.start()
        for put in puts:
            put.wait()

    out = pl.pallas_call(
        kernel,
        out_shape=[jax.ShapeDtypeStruct((size,) + tail, array.dtype) for size in sizes]
        + [
            jax.ShapeDtypeStruct((sources * points, 2 * stations * points), BF16),
            jax.ShapeDtypeStruct((width + 2 * LANES, width), BF16),
            jax.ShapeDtypeStruct((2, points, 2 * points), BF16),
        ],
        in_specs=[SMEM, SMEM, SMEM, ANY],
        out_specs=[ANY] * pieces + [VMEM] * 3,
        scratch_shapes=[pltpu.VMEM(array.shape[:1] + tail, array.dtype), pltpu.SemaphoreType.DMA((2, pieces))],
        name="prepare",
    )(block.reshape(1), filters, pairs, array)
    return out[:pieces], out[pieces:]


def local_kernel(
    block_ref, mix_ref, dcol_ref, drow_ref, green_ref, left_ref, mid_ref, right_ref, lam_ref, mu_ref,
    *rest, last_block, waits, more,
):
    added = rest[waits : waits + more]
    part_ref, z_ref, gs, xs, ys = rest[waits + more :]
    snaps = z_ref.shape[2]
    rows, width = z_ref.shape[-2:]
    stations = green_ref.shape[0]
    half = rows // 2
    points = snaps * half
    span = lambda h: pl.ds(h * half, half)

    def filtered(*accs):
        k = 0
        for h in range(2):
            for c in range(0, 6, 2):
                for unit in range(2):
                    tile = green_ref[:, :, c + unit, 0, span(h)].reshape(stations * points, width)
                    pltpu.matmul_push_rhs(tile, staging_register=k % 2, mxu_index=unit)
                for part in range(2):
                    lhs = mix_ref[:, pl.ds(part * stations * points, stations * points)]
                    for unit in range(2):
                        acc = accs[2 * unit + k % 2]
                        pltpu.matmul_acc_lhs(acc, lhs, load_staged_rhs=k % 2 if part == 0 else None)
                for unit in range(2):
                    gs[c + unit, h] = pltpu.matmul_pop(accs[2 * unit + k % 2])
                k += 1

    block = block_ref[0]
    whole, ends = [], []
    for i in range(3):
        whole.append(mid_ref[0, :, i, 0].reshape(2 * points, width))
        left = left_ref[0, :, i, 0]
        right = right_ref[0, :, i, 0]
        left = jnp.where(block == 0, jnp.zeros_like(left), left)
        right = jnp.where(block == last_block, jnp.zeros_like(right), right)
        ends.append(jnp.concatenate([left, right], axis=2).reshape(2 * points, width))

    def columns(*accs):
        for tile, lhs in enumerate((whole, ends)):
            for unit in range(2):
                pltpu.matmul_push_rhs(dcol_ref[pl.ds(tile * width, width)], staging_register=tile, mxu_index=unit)
            for unit in range(2):
                pltpu.matmul_acc_lhs(accs[2 * unit], lhs[unit], load_staged_rhs=tile)
                pltpu.matmul_acc_lhs(accs[2 * unit + 1], lhs[2][unit * points : (unit + 1) * points])
        for unit in range(2):
            xs[unit] = pltpu.matmul_pop(accs[2 * unit])
            xs[2, pl.ds(unit * points, points)] = pltpu.matmul_pop(accs[2 * unit + 1])

    def lines(*accs):
        for unit in range(2):
            pltpu.matmul_push_rhs(whole[unit], staging_register=0, mxu_index=unit)
            pltpu.matmul_push_rhs(whole[2], staging_register=1, mxu_index=unit)
        for unit in range(2):
            pltpu.matmul_acc_lhs(accs[3 * unit], drow_ref[0], load_staged_rhs=0)
            pltpu.matmul_acc_lhs(accs[3 * unit + 1], drow_ref[1])
            pltpu.matmul_acc_lhs(accs[3 * unit + 2], drow_ref[unit], load_staged_rhs=1)
        for unit in range(2):
            ys[unit, 0] = pltpu.matmul_pop(accs[3 * unit])
            ys[unit, 1] = pltpu.matmul_pop(accs[3 * unit + 1])
            ys[2, unit] = pltpu.matmul_pop(accs[3 * unit + 2])

    space = lambda unit, size: pltpu.ACC(unit)((size, width), F32)
    pl.run_scoped(filtered, *[space(unit, points) for unit in range(2) for _ in range(2)])
    pl.run_scoped(columns, *[space(unit, size) for unit in range(2) for size in (2 * points, points)])
    pl.run_scoped(lines, *[space(unit, points) for unit in range(2) for _ in range(3)])

    zero = jnp.zeros((half, width), F32)
    for h in range(2):
        lam = lam_ref[0, span(h)]
        mu2 = 2.0 * mu_ref[0, span(h)]

        def step(s, carry):
            vol, dev = carry
            at = pl.ds(pl.multiple_of(s * half, half), half)
            full = pl.ds(pl.multiple_of((2 * s + h) * half, half), half)
            gxx, gyy, gzz, gyz, gxz, gxy = (gs[c, h, at] for c in range(6))
            gtr = gxx + gyy + gzz
            dxx, dyy = xs[0, full], ys[1, h, at]
            vol = vol + (dxx + dyy) * gtr
            dev = dev + (dxx * gxx + dyy * gyy) + (ys[2, h, at] * gyz + xs[2, full] * gxz)
            dev = dev + (xs[1, full] + ys[0, h, at]) * gxy
            for i, z in enumerate((mu2 * gxz, mu2 * gyz, lam * gtr + mu2 * gzz)):
                for ref in added:
                    z = z + ref[0, i, s, 0, span(h)].astype(F32)
                z_ref[0, i, s, 0, span(h)] = z.astype(BF16)
            return vol, dev

        vol, dev = lax.fori_loop(0, snaps, step, (zero, zero), unroll=4)
        part_ref[0, 0, span(h)] = (lam * vol + mu2 * dev) / 12.0


def local_terms(block, first, count, mats, green, displacement, lam, mu, width, after=(), add=()):
    _, snaps, _, planes, rows, cols = displacement.shape
    stations = green.shape[0]
    points = snaps * rows
    per = width // LANES
    top = cols // LANES - 1
    mix, dcol, drow = mats
    g_at = lambda e, z, b: (0, 0, 0, z, 0, b[0])
    u_at = lambda f: (lambda e, z, b: (first + e, 0, 0, z, 0, f(b[0])))
    m_at = lambda e, z, b: (z, 0, b[0])
    z_spec = pl.BlockSpec((1, 3, snaps, 1, rows, width), lambda e, z, b: (e, 0, 0, z, 0, 0))
    return pl.pallas_call(
        functools.partial(local_kernel, last_block=cols // width - 1, waits=len(after), more=len(add)),
        out_shape=(
            jax.ShapeDtypeStruct((count, planes, rows, width), F32),
            jax.ShapeDtypeStruct((count, 3, snaps, planes, rows, width), BF16),
        ),
        grid_spec=pltpu.PrefetchScalarGridSpec(
            num_scalar_prefetch=1,
            grid=(count, planes),
            in_specs=[
                pl.BlockSpec((points // 2, mix.shape[1]), lambda e, z, b: (first + e, 0)),
                pl.BlockSpec(dcol.shape, lambda e, z, b: (0, 0)),
                pl.BlockSpec(drow.shape, lambda e, z, b: (0, 0, 0)),
                pl.BlockSpec((stations, snaps, 6, 1, rows, width), g_at),
                pl.BlockSpec((1, snaps, 3, 1, rows, LANES), u_at(lambda b: jnp.maximum(per * b - 1, 0))),
                pl.BlockSpec((1, snaps, 3, 1, rows, width), u_at(lambda b: b)),
                pl.BlockSpec((1, snaps, 3, 1, rows, LANES), u_at(lambda b: jnp.minimum(per * b + per, top))),
                pl.BlockSpec((1, rows, width), m_at),
                pl.BlockSpec((1, rows, width), m_at),
            ]
            + [ANY] * len(after)
            + [z_spec] * len(add),
            out_specs=(pl.BlockSpec((1, 1, rows, width), lambda e, z, b: (e, z, 0, 0)), z_spec),
            scratch_shapes=[
                pltpu.VMEM((6, 2, points // 2, width), F32),
                pltpu.VMEM((3, points, width), F32),
                pltpu.VMEM((3, 2, points // 2, width), F32),
            ],
        ),
        cost_estimate=pl.CostEstimate(
            flops=int(count * planes * 2 * width * points * (6 * stations * points + 3 * 2 * width + 3 * points)),
            bytes_accessed=int(count * planes * width * rows * snaps * (6 * stations + 9) * 2),
            transcendentals=0,
        ),
        name="local_terms",
    )(block.reshape(1), mix, dcol, drow, green, displacement, displacement, displacement, lam, mu, *after, *add)


def depth_kernel(coef_ref, own_ref, near_ref, far_ref, z0_ref, z1_ref, old_ref, new_ref):
    snaps = own_ref.shape[0]

    def step(s, carry):
        top, bottom = carry
        for i in range(3):
            own0, own1 = own_ref[s, i, 0].astype(F32), own_ref[s, i, 1].astype(F32)
            n0, n1 = near_ref[s, i, 0].astype(F32), near_ref[s, i, 1].astype(F32)
            f0, f1 = far_ref[s, i, 0].astype(F32), far_ref[s, i, 1].astype(F32)
            d0 = 8.0 * own1 + (coef_ref[0] * n0 + coef_ref[1] * n1) + (coef_ref[2] * f0 + coef_ref[3] * f1)
            d1 = (coef_ref[4] * n0 + coef_ref[5] * n1) + (coef_ref[6] * f0 + coef_ref[7] * f1) - 8.0 * own0
            z = [z0_ref[0, i, s, p].astype(F32) + z1_ref[0, i, s, p].astype(F32) for p in range(2)]
            top = top + z[0] * d0
            bottom = bottom + z[1] * d1
        return top, bottom

    zero = jnp.zeros(new_ref.shape[1:], F32)
    top, bottom = lax.fori_loop(0, snaps, step, (zero, zero), unroll=2)

    @pl.when(pl.program_id(0) == 0)
    def _():
        new_ref[...] = old_ref[...]

    new_ref[0] += top / 12.0
    new_ref[1] += bottom / 12.0


def depth_terms(coefs, own, near, far, z0, z1, old, source, at, lead, count, unit):
    comps, planes, rows, width = own.shape[1:]
    whole = pl.BlockSpec(old.shape, lambda s: (0,) * old.ndim)
    u_spec = pl.BlockSpec((unit,) + own.shape[1:], lambda s: (lead // unit + s, 0, 0, 0, 0))
    z_spec = lambda e: pl.BlockSpec((1, comps, unit, planes, rows, width), lambda s: (e, 0, at // unit + s, 0, 0, 0))
    return pl.pallas_call(
        depth_kernel,
        out_shape=jax.ShapeDtypeStruct((planes, rows, width), F32),
        grid=(count // unit,),
        in_specs=[SMEM] + [u_spec] * 3 + [z_spec(source), z_spec(0), whole],
        out_specs=whole,
        name="depth_terms",
    )(coefs, own, near, far, z0, z1, old)


def cut_kernel(me_ref, *refs, groups):
    total, outs, held = refs[: -groups - 1], refs[-groups - 1 : -1], refs[-1]
    part = outs[0].shape[2]
    for q in range(groups):
        for e, ref in enumerate(total):
            held[q, e] = ref[:, q * part : (q + 1) * part, :]
    for bits, out in enumerate(outs):
        out[...] = held[me_ref[0] ^ bits]


def cut_rows(me, totals, groups):
    planes, rows, width = totals[0].shape
    shape = (len(totals), planes, rows // groups, width)
    return pl.pallas_call(
        functools.partial(cut_kernel, groups=groups),
        out_shape=[jax.ShapeDtypeStruct(shape, F32)] * groups,
        in_specs=[SMEM] + [VMEM] * len(totals),
        out_specs=[VMEM] * groups,
        scratch_shapes=[pltpu.VMEM((groups,) + shape, F32)],
        name="cut_rows",
    )(me.reshape(1), *totals)


def spread_kernel(me_ref, *refs, groups, counts):
    ins, outs, held = refs[: -groups - 1], refs[-groups - 1 : -1], refs[-1]
    part = outs[0].shape[2]
    at = 0
    for bits, count in enumerate(counts):
        e = 0
        for ref in ins[at : at + count]:
            width = ref.shape[-1]
            columns = pl.ds(pl.multiple_of((me_ref[0] ^ bits) * width, width), width)
            for k in range(ref.shape[0]):
                for q in range(groups):
                    held[q, e, :, :, columns] = ref[k, :, q * part : (q + 1) * part, :]
                e += 1
        at += count
    for bits, out in enumerate(outs):
        out[...] = held[me_ref[0] ^ bits]


def spread_rows(me, blocks, groups):
    planes, rows, width = blocks[0][0].shape[1:]
    sources = sum(piece.shape[0] for piece in blocks[0])
    shape = (sources, planes, rows // groups, width * len(blocks))
    flat = [piece for pieces in blocks for piece in pieces]
    return pl.pallas_call(
        functools.partial(spread_kernel, groups=groups, counts=[len(pieces) for pieces in blocks]),
        out_shape=[jax.ShapeDtypeStruct(shape, F32)] * groups,
        in_specs=[SMEM] + [VMEM] * len(flat),
        out_specs=[VMEM] * groups,
        scratch_shapes=[pltpu.VMEM((groups,) + shape, F32)],
        name="spread_rows",
    )(me.reshape(1), *flat)


def join_kernel(me_ref, base_ref, *refs):
    pieces, out = refs[:-1], refs[-1]
    width = pieces[0].shape[-1]
    for bits, piece in enumerate(pieces):
        columns = pl.ds(pl.multiple_of((me_ref[0] ^ bits) * width, width), width)
        out[..., columns] = base_ref[..., columns] + piece[...]


def join_columns(me, base, pieces):
    return pl.pallas_call(
        join_kernel,
        out_shape=jax.ShapeDtypeStruct(base.shape, F32),
        in_specs=[SMEM] + [VMEM] * (len(pieces) + 1),
        out_specs=VMEM,
        name="join_columns",
    )(me.reshape(1), base, *pieces)


SHARES = (1, 2, 2, 2, 1)


def on_device(displacement, green, lame_lambda, shear_modulus, filters, pairs):
    sources, snaps, _, planes, rows, cols = displacement.shape
    groups = lax.axis_size("rcv")
    slabs = lax.axis_size("slab")
    me = lax.axis_index("rcv")
    slab = lax.axis_index("slab")
    width = cols // groups
    pair_swap = [(i, i ^ 1) for i in range(slabs)]
    onward = [(i, i + 2 if i % 2 == 0 else i - 2) for i in range(slabs)]
    onward = [(i, j) for i, j in onward if 0 <= j < slabs]

    def swap(x, bit):
        return lax.ppermute(x, "rcv", [(i, i ^ bit) for i in range(groups)])

    def along(x, links):
        return lax.ppermute(x, "slab", links)

    def terms(bits, first, count, after=(), add=()):
        return local_terms(
            me ^ bits, first, count, mats, green, displacement, lame_lambda, shear_modulus, width, after, add
        )

    total_snaps = sources * snaps
    unit = total_snaps // sum(SHARES)
    sizes = [share * unit for share in SHARES]
    lead = displacement.reshape((total_snaps,) + displacement.shape[2:])
    own, mats = prepare(lead, me, width, sizes, filters, pairs, snaps)
    near = [along(piece, pair_swap) for piece in own]
    far = [along(piece, onward) for piece in near]

    across, parts = [], [[] for _ in range(groups)]
    last = own[0]
    sent = []
    for e in range(sources):
        part, last = terms(3, e, 1, (last,))
        parts[3].append(part)
        sent.append(swap(last, 1))
    for e in range(sources):
        part, last = terms(2, e, 1, (last,), (sent[e],))
        parts[2].append(part)
        across.append(swap(last, 2))
    part, last = terms(1, 0, sources, (last,))
    parts[1].append(part)
    part, z0 = terms(0, 0, sources, (last,), (swap(last, 1),))
    parts[0].append(part)
    base = spread_rows(me, parts, groups)
    base = sum([base[0]] + [swap(base[bits], bits) for bits in range(1, groups)])

    even = slab % 2 == 0
    coefs = jnp.where(
        even,
        jnp.array([-1, 0, 1, -8, 8, -1, 0, 1], F32),
        jnp.array([1, -8, -1, 0, 0, 1, 8, -1], F32),
    )
    totals = [jnp.zeros((planes, rows, width), F32)] * sources
    begin = 0
    for k, size in enumerate(sizes):
        at = begin
        while at < begin + size:
            e = at // snaps
            count = min(begin + size, (e + 1) * snaps) - at
            totals[e] = depth_terms(
                coefs, own[k], near[k], far[k], z0, across[e], totals[e], e, at % snaps, at - begin, count, unit
            )
            at += count
        begin += size
    pieces = cut_rows(me, totals, groups)
    pieces = [piece if bits == 0 else swap(piece, bits) for bits, piece in enumerate(pieces)]
    return join_columns(me, base, pieces)


def solution(mesh):
    placed = (
        P(None, None, None, "slab", None, None),
        P("rcv", None, None, "slab", None, None),
        P("slab", None, None),
        P("slab", None, None),
        P(None, "rcv", None),
        P(None, "rcv"),
    )
    return jax.shard_map(
        on_device,
        mesh=mesh,
        in_specs=placed,
        out_specs=P(None, "slab", "rcv", None),
        check_vma=False,
    )
```

```python
import functools
import jax
import jax.numpy as jnp
import numpy as np
from jax import lax
from jax.experimental import pallas as pl
from jax.experimental.pallas import tpu as pltpu
from jax.sharding import PartitionSpec as P

LANES = 128
F32 = jnp.float32
BF16 = jnp.bfloat16
ANY = pl.BlockSpec(memory_space=pl.ANY)
SMEM = pl.BlockSpec(memory_space=pltpu.SMEM)
VMEM = pl.BlockSpec(memory_space=pltpu.VMEM)


def stencil(offset):
    return 8.0 * (offset == 1) - 8.0 * (offset == -1) - 1.0 * (offset == 2) + 1.0 * (offset == -2)


def stencils(snaps, rows, width):
    place = np.arange(width)
    dcol = stencil(place[:, None] - place[None, :])
    snap = np.arange(snaps)
    same = snap[:, None] == snap[None, :]
    drow = []
    for h in range(2):
        row = np.arange(rows // 2) + h * (rows // 2)
        band = stencil(np.arange(rows)[None, :] - row[:, None])
        drow.append(np.kron(same, band))
    return jnp.asarray(dcol, BF16), jnp.asarray(np.stack(drow), BF16)


def iota(shape, axis):
    return lax.broadcasted_iota(jnp.int32, shape, axis)


def in_vmem(x):
    return pltpu.with_memory_space_constraint(x, pltpu.VMEM)


def in_hbm(x):
    return pltpu.with_memory_space_constraint(x, pltpu.HBM)


def two_parts(high, low):
    return high.astype(F32) + low.astype(F32)


def over(x, n):
    if n & (n - 1):
        return lax.div(x, jnp.int32(n)), lax.rem(x, jnp.int32(n))
    return lax.shift_right_logical(x, jnp.int32(n.bit_length() - 1)), x & jnp.int32(n - 1)


def mm(a, b):
    return jnp.dot(a, b, preferred_element_type=F32)


def fill_mix(filters_ref, pairs_ref, mix_ref, rows):
    sources, stations, lags = filters_ref.shape
    points = mix_ref.shape[0] // sources
    snaps = points // rows
    depth = mix_ref.shape[1]
    shape = (snaps, stations * snaps)
    station, at = over(iota(shape, 1), snaps)
    lag = iota(shape, 0) - at + lags // 2
    spread = (over(iota((points, snaps), 0), rows)[0] == iota((points, snaps), 1)).astype(BF16)
    fan = (over(iota((depth // rows, depth), 1), rows)[0] == iota((depth // rows, depth), 0)).astype(BF16)
    same = over(iota((points, depth), 0), rows)[1] == over(iota((points, depth), 1), rows)[1]
    for e in range(sources):
        table = jnp.zeros(shape, F32)
        for r in range(stations):
            used = pairs_ref[e, r].astype(F32)
            for j in range(lags):
                table = jnp.where((station == r) & (lag == j), used * filters_ref[e, r, j], table)
        high = table.astype(BF16)
        low = (table - high.astype(F32)).astype(BF16)
        taps = jnp.concatenate([high, low], axis=1)
        full = mm(mm(spread, taps).astype(BF16), fan)
        mix_ref[pl.ds(e * points, points)] = jnp.where(same, full, 0.0).astype(BF16)


def prepare(displacement, lam, mu, me, slab, width, sizes, filters, pairs):
    sources, snaps, comps, planes, rows, _ = displacement.shape
    stations = filters.shape[1]
    points = snaps * rows // 2
    pieces = len(sizes)
    marks = [divmod(sum(sizes[:k]), snaps) for k in range(pieces)]
    fixed = stencils(snaps, rows, width)

    def kernel(me_ref, slab_ref, filters_ref, pairs_ref, src, *rest):
        ins, outs, (u_ref, *copies), mix_ref, sems = rest[:4], rest[4 : 4 + pieces], rest[4 + pieces : -2], rest[-2], rest[-1]
        here = pl.ds(pl.multiple_of(me_ref[0] * width, width), width)
        spans = [(e, pl.ds(s, size)) for (e, s), size in zip(marks, sizes)]
        gets = [pltpu.make_async_copy(src.at[span], u_ref.at[span], sems.at[0, k]) for k, span in enumerate(spans)]
        puts = [
            pltpu.make_async_copy(u_ref.at[span + (slice(None),) * 3 + (here,)], outs[k], sems.at[1, k])
            for k, span in enumerate(spans)
        ]
        others = [pltpu.make_async_copy(a, b, sems.at[2, k]) for k, (a, b) in enumerate(zip(ins, copies))]
        for copy in gets + others:
            copy.start()
        fill_mix(filters_ref, pairs_ref, mix_ref, rows // 2)
        for get, put in zip(gets, puts):
            get.wait()
            put.start()
        for copy in others + puts:
            copy.wait()

    hbm = (lam, mu) + fixed
    out = pl.pallas_call(
        kernel,
        out_shape=[jax.ShapeDtypeStruct((size, comps, planes, rows, width), displacement.dtype) for size in sizes]
        + [pltpu.VMEM(array.shape, array.dtype) for array in (displacement,) + hbm]
        + [pltpu.VMEM((sources * points, 4 * stations * points // 2), BF16)],
        in_specs=[SMEM] * 4 + [ANY] * 5,
        out_specs=[ANY] * pieces + [VMEM] * 6,
        scratch_shapes=[pltpu.SemaphoreType.DMA((3, max(pieces, 4)))],
        cost_estimate=pl.CostEstimate(
            flops=0, bytes_accessed=int(8 * displacement.size * displacement.dtype.itemsize), transcendentals=0
        ),
        compiler_params=pltpu.CompilerParams(vmem_limit_bytes=8 * 2**20),
        name="prepare",
    )(me, slab, in_hbm(filters), in_hbm(pairs), in_hbm(displacement), *map(in_hbm, hbm))
    pieces_out, (u, lam, mu, dcol, drow, mix) = out[:pieces], out[pieces:]
    return pieces_out, (mix, dcol, drow), u, lam, mu


def local_kernel(
    me_ref, mix_ref, dcol_ref, drow_ref, green_ref, u_ref, lam_ref, mu_ref, *rest, bits, first, waits, more
):
    added = rest[waits : waits + more]
    z_ref, gs, xs, ys = rest[waits + more :]
    count, _, planes, rows, width = z_ref.shape
    stations, snaps = green_ref.shape[:2]
    cols = u_ref.shape[-1]
    half = rows // 2
    points = snaps * half
    block = me_ref[0] ^ bits
    here = pl.ds(pl.multiple_of(block * width, width), width)
    before = pl.ds(pl.multiple_of(jnp.maximum(block * width - LANES, 0), LANES), LANES)
    behind = pl.ds(pl.multiple_of(jnp.minimum(block * width + width, cols - LANES), LANES), LANES)
    span = lambda h: pl.ds(h * half, half)
    space = lambda unit, size: pltpu.ACC(unit)((size, width), F32)

    lane = iota((half, LANES), 1)
    inner_left = jnp.where(block == 0, 0.0, 1.0)
    inner_right = jnp.where(block == cols // width - 1, 0.0, 1.0)
    left_2 = jnp.where(lane < 2, 1.0, 0.0) * inner_left
    left_1 = jnp.where(lane == 0, -8.0, 0.0) * inner_left
    right_2 = jnp.where(lane >= LANES - 2, -1.0, 0.0) * inner_right
    right_1 = jnp.where(lane == LANES - 1, 8.0, 0.0) * inner_right

    def one(index, carry):
        now, e = over(index, count)
        quake = first + e

        def filtered(h):
            def run(*accs):
                for k in range(3):
                    for unit in range(2):
                        tile = green_ref[:, :, 2 * k + unit, now, span(h), here].reshape(stations * points, width)
                        pltpu.matmul_push_rhs(tile, staging_register=k % 2, mxu_index=unit)
                    for part in range(2):
                        row = pl.ds(pl.multiple_of(quake * points, points), points)
                        lhs = mix_ref[row, pl.ds(part * stations * points, stations * points)]
                        for unit in range(2):
                            acc = accs[2 * unit + k % 2]
                            pltpu.matmul_acc_lhs(acc, lhs, load_staged_rhs=k % 2 if part == 0 else None)
                    for unit in range(2):
                        gs[2 * k + unit, h] = pltpu.matmul_pop(accs[2 * unit + k % 2])

            pl.run_scoped(run, *[space(unit, points) for unit in range(2) for _ in range(2)])

        whole = [u_ref[quake, :, i, now, :, here].reshape(2 * points, width) for i in range(3)]

        def columns(*accs):
            for unit in range(2):
                pltpu.matmul_push_rhs(dcol_ref[...], staging_register=0, mxu_index=unit)
            for unit in range(2):
                pltpu.matmul_acc_lhs(accs[2 * unit], whole[unit], load_staged_rhs=0)
                pltpu.matmul_acc_lhs(accs[2 * unit + 1], whole[2][unit * points : (unit + 1) * points])
            for unit in range(2):
                xs[unit] = pltpu.matmul_pop(accs[2 * unit])
                xs[2, pl.ds(unit * points, points)] = pltpu.matmul_pop(accs[2 * unit + 1])

        def lines(*accs):
            for unit in range(2):
                pltpu.matmul_push_rhs(whole[unit], staging_register=0, mxu_index=unit)
                pltpu.matmul_push_rhs(whole[2], staging_register=1, mxu_index=unit)
            for unit in range(2):
                pltpu.matmul_acc_lhs(accs[3 * unit], drow_ref[0], load_staged_rhs=0)
                pltpu.matmul_acc_lhs(accs[3 * unit + 1], drow_ref[1])
                pltpu.matmul_acc_lhs(accs[3 * unit + 2], drow_ref[unit], load_staged_rhs=1)
            for unit in range(2):
                ys[unit, 0] = pltpu.matmul_pop(accs[3 * unit])
                ys[unit, 1] = pltpu.matmul_pop(accs[3 * unit + 1])
                ys[2, unit] = pltpu.matmul_pop(accs[3 * unit + 2])

        def along_columns(i, s, h):
            left = u_ref[quake, s, i, now, span(h), before].astype(F32)
            right = u_ref[quake, s, i, now, span(h), behind].astype(F32)
            left = pltpu.roll(left, 2, 1) * left_2 + pltpu.roll(left, 1, 1) * left_1
            right = pltpu.roll(right, LANES - 2, 1) * right_2 + pltpu.roll(right, LANES - 1, 1) * right_1
            inside = xs[i, pl.ds((2 * s + h) * half, half)]
            middle = inside[:, LANES : width - LANES]
            parts = [inside[:, :LANES] + left] + ([middle] if middle.shape[1] else [])
            return jnp.concatenate(parts + [inside[:, width - LANES :] + right], axis=1)

        def combine(h):
            vol = dev = jnp.zeros((half, width), F32)
            lam = lam_ref[now, span(h), here]
            mu2 = 2.0 * mu_ref[now, span(h), here]
            for s in range(snaps):
                at = pl.ds(s * half, half)
                xs0, xs1, xs2 = (along_columns(i, s, h) for i in range(3))
                gxx, gyy, gzz, gyz, gxz, gxy = (gs[c, h, at] for c in range(6))
                gtr = gxx + gyy + gzz
                dxx, dyy = xs0, ys[1, h, at]
                vol = vol + (dxx + dyy) * gtr
                dev = dev + (dxx * gxx + dyy * gyy) + (ys[2, h, at] * gyz + xs2 * gxz)
                dev = dev + (xs1 + ys[0, h, at]) * gxy
                for i, z in enumerate((mu2 * gxz, mu2 * gyz, lam * gtr + mu2 * gzz)):
                    for ref in added:
                        z = z + ref[e, i * snaps + s, now, span(h)].astype(F32)
                    z_ref[e, i * snaps + s, now, span(h)] = z.astype(BF16)
            part = (lam * vol + mu2 * dev) / 12.0
            for ref in added:
                part = part + two_parts(ref[e, 3 * snaps, now, span(h)], ref[e, 3 * snaps + 1, now, span(h)])
            high = part.astype(BF16)
            z_ref[e, 3 * snaps, now, span(h)] = high
            z_ref[e, 3 * snaps + 1, now, span(h)] = (part - high.astype(F32)).astype(BF16)

        pl.run_scoped(columns, *[space(unit, size) for unit in range(2) for size in (2 * points, points)])
        pl.run_scoped(lines, *[space(unit, points) for unit in range(2) for _ in range(3)])
        filtered(0)
        filtered(1)
        combine(0)
        combine(1)
        return carry

    lax.fori_loop(0, planes * count, one, 0)


def local_terms(me, bits, first, count, mats, green, displacement, lam, mu, width, after=(), add=()):
    _, snaps, _, planes, rows, _ = displacement.shape
    stations = green.shape[0]
    points = snaps * rows
    return pl.pallas_call(
        functools.partial(local_kernel, bits=bits, first=first, waits=len(after), more=len(add)),
        out_shape=jax.ShapeDtypeStruct((count, 3 * snaps + 2, planes, rows, width), BF16),
        in_specs=[SMEM] + [VMEM] * 7 + [ANY] * len(after) + [VMEM] * len(add),
        out_specs=VMEM,
        scratch_shapes=[
            pltpu.VMEM((6, 2, points // 2, width), F32),
            pltpu.VMEM((3, points, width), F32),
            pltpu.VMEM((3, 2, points // 2, width), F32),
        ],
        cost_estimate=pl.CostEstimate(
            flops=int(count * planes * 2 * width * points * (6 * stations * points + 3 * width + 3 * points)),
            bytes_accessed=int(count * planes * width * rows * snaps * (6 * stations + 9) * 2),
            transcendentals=0,
        ),
        compiler_params=pltpu.CompilerParams(vmem_limit_bytes=16 * 2**20),
        name="local_terms",
    )(me, *mats, in_vmem(green), displacement, lam, mu, *after, *map(in_vmem, add))


def depth_kernel(me_ref, slab_ref, *refs, groups, slabs, lasts):
    pieces, rest = refs[:lasts[0]], refs[lasts[0] :]
    z0_ref, z1_ref, outs = rest[0], rest[1], rest[2:]
    _, rows, width = z1_ref.shape[2:]
    source = lasts[1]
    snaps = (z1_ref.shape[1] - 2) // 3
    slab = slab_ref[0]
    even = slab % 2 == 0
    known = jnp.where(even, slab > 0, slab < slabs - 1).astype(F32)
    pick = lambda one, other: jnp.where(even, jnp.float32(one), jnp.float32(other))
    coefs = [pick(*both) for both in ((-1, 1), (0, -8), (1, -1), (-8, 0), (8, 0), (-1, 1), (0, 8), (1, -1))]
    coefs = [coef * known if k % 4 >= 2 else coef for k, coef in enumerate(coefs)]
    total = [
        sum(two_parts(ref[k, 3 * snaps, p], ref[k, 3 * snaps + 1, p]) for ref, k in ((z0_ref, source), (z1_ref, 0)))
        for p in range(2)
    ]
    carry = tuple(jnp.zeros((rows, width), F32) for _ in range(2))
    at = 0
    for own_ref, near_ref, far_ref in zip(pieces[0::3], pieces[1::3], pieces[2::3]):

        def step(s, carry, at=at, own_ref=own_ref, near_ref=near_ref, far_ref=far_ref):
            top, bottom = carry
            for i in range(3):
                own0, own1 = own_ref[s, i, 0].astype(F32), own_ref[s, i, 1].astype(F32)
                n0, n1 = near_ref[s, i, 0].astype(F32), near_ref[s, i, 1].astype(F32)
                f0, f1 = far_ref[s, i, 0].astype(F32), far_ref[s, i, 1].astype(F32)
                d0 = 8.0 * own1 + (coefs[0] * n0 + coefs[1] * n1) + (coefs[2] * f0 + coefs[3] * f1)
                d1 = (coefs[4] * n0 + coefs[5] * n1) + (coefs[6] * f0 + coefs[7] * f1) - 8.0 * own0
                k = i * snaps + at + s
                z = [z0_ref[source, k, p].astype(F32) + z1_ref[0, k, p].astype(F32) for p in range(2)]
                top = top + z[0] * d0
                bottom = bottom + z[1] * d1
            return top, bottom

        count = own_ref.shape[0]
        carry = lax.fori_loop(0, count, step, carry, unroll=2)
        at += count
    part = rows // groups
    held = outs[-1]
    for p in range(2):
        value = total[p] + carry[p] / 12.0
        for q in range(groups):
            held[q, p] = value[q * part : (q + 1) * part]
    for bits, out in enumerate(outs[:-1]):
        out[...] = held[me_ref[0] ^ bits]


def depth_terms(me, slab, pieces, z0, z1, source, groups, slabs):
    planes, rows, width = z1.shape[2:]
    shape = (planes, rows // groups, width)
    flat = [array for piece in pieces for array in piece]
    return pl.pallas_call(
        functools.partial(depth_kernel, groups=groups, slabs=slabs, lasts=(len(flat), source)),
        out_shape=[jax.ShapeDtypeStruct(shape, F32)] * groups,
        in_specs=[SMEM, SMEM] + [VMEM] * (len(flat) + 2),
        out_specs=[VMEM] * groups,
        scratch_shapes=[pltpu.VMEM((groups,) + shape, F32)],
        compiler_params=pltpu.CompilerParams(vmem_limit_bytes=8 * 2**20),
        name="depth_terms",
    )(me, slab, *map(in_vmem, flat + [z0, z1]))


def join_kernel(me_ref, *refs):
    pieces, out = refs[:-1], refs[-1]
    sources = out.shape[0]
    width = pieces[0].shape[-1]
    for k, piece in enumerate(pieces):
        bits, e = divmod(k, sources)
        out[e, :, :, pl.ds(pl.multiple_of((me_ref[0] ^ bits) * width, width), width)] = piece[...]


def join_columns(me, pieces, sources):
    planes, part, width = pieces[0].shape
    return pl.pallas_call(
        join_kernel,
        out_shape=jax.ShapeDtypeStruct((sources, planes, part, width * len(pieces) // sources), F32),
        in_specs=[SMEM] + [VMEM] * len(pieces),
        out_specs=VMEM,
        compiler_params=pltpu.CompilerParams(vmem_limit_bytes=8 * 2**20),
        name="join_columns",
    )(me, *map(in_vmem, pieces))


SHARES = (1, 1, 1, 1)


def on_device(displacement, green, lame_lambda, shear_modulus, filters, pairs):
    sources, snaps, _, _, _, cols = displacement.shape
    groups = lax.axis_size("rcv")
    slabs = lax.axis_size("slab")
    me = lax.axis_index("rcv").reshape(1)
    slab = lax.axis_index("slab").reshape(1)
    width = cols // groups
    pair_swap = [(i, i ^ 1) for i in range(slabs)]
    onward = [(i, (i + 2 if i % 2 == 0 else i - 2) % slabs) for i in range(slabs)]

    def swap(x, bit):
        return lax.ppermute(x, "rcv", [(i, i ^ bit) for i in range(groups)])

    def along(x, links):
        return lax.ppermute(x, "slab", links)

    def terms(bits, first, count, after=(), add=()):
        return local_terms(
            me, bits, first, count, mats, green, u, lam, mu, width, after, add
        )

    total_snaps = sources * snaps
    unit = total_snaps // sum(SHARES)
    sizes = [share * unit for share in SHARES]
    own, mats, u, lam, mu = prepare(displacement, lame_lambda, shear_modulus, me, slab, width, sizes, filters, pairs)
    near = [along(piece, pair_swap) for piece in own]
    far = [along(piece, onward) for piece in near]

    across = []
    last = own[0]
    for e in range(sources):
        last = terms(3, e, 1, (last,))
        sent = swap(last, 1)
        last = terms(2, e, 1, (last,), (sent,))
        across.append(swap(last, 2))
    last = terms(1, 0, sources, (last,))
    z0 = terms(0, 0, sources, (last,), (swap(last, 1),))

    pieces = []
    for e in range(sources):
        mine = [k for k in range(len(SHARES)) if sum(sizes[:k]) // snaps == e]
        pieces.append(depth_terms(me, slab, [(own[k], near[k], far[k]) for k in mine], z0, across[e], e, groups, slabs))
    ends = []
    for bits in range(groups):
        for e in range(sources):
            piece = pieces[e][bits]
            ends.append(swap(piece, bits) if bits else piece)
    return join_columns(me, ends, sources)


def solution(mesh):
    placed = (
        P(None, None, None, "slab", None, None),
        P("rcv", None, None, "slab", None, None),
        P("slab", None, None),
        P("slab", None, None),
        P(None, "rcv", None),
        P(None, "rcv"),
    )
    return jax.shard_map(
        on_device,
        mesh=mesh,
        in_specs=placed,
        out_specs=P(None, "slab", "rcv", None),
        check_vma=False,
    )
```

```python
import functools
import jax
import jax.numpy as jnp
import numpy as np
from jax import lax
from jax.experimental import pallas as pl
from jax.experimental.pallas import tpu as pltpu
from jax.sharding import PartitionSpec as P

LANES = 128
F32 = jnp.float32
BF16 = jnp.bfloat16
ANY = pl.BlockSpec(memory_space=pl.ANY)
SMEM = pl.BlockSpec(memory_space=pltpu.SMEM)
VMEM = pl.BlockSpec(memory_space=pltpu.VMEM)


def stencil(offset):
    return 8.0 * (offset == 1) - 8.0 * (offset == -1) - 1.0 * (offset == 2) + 1.0 * (offset == -2)


def stencils(snaps, rows, width):
    place = np.arange(width)
    dcol = stencil(place[:, None] - place[None, :])
    snap = np.arange(snaps)
    same = snap[:, None] == snap[None, :]
    drow = []
    for h in range(2):
        row = np.arange(rows // 2) + h * (rows // 2)
        band = stencil(np.arange(rows)[None, :] - row[:, None])
        drow.append(np.kron(same, band))
    return jnp.asarray(dcol, BF16), jnp.asarray(np.stack(drow), BF16)


def iota(shape, axis):
    return lax.broadcasted_iota(jnp.int32, shape, axis)


def in_vmem(x):
    return pltpu.with_memory_space_constraint(x, pltpu.VMEM)


def in_hbm(x):
    return pltpu.with_memory_space_constraint(x, pltpu.HBM)


def two_parts(high, low):
    return high.astype(F32) + low.astype(F32)


def over(x, n):
    if n & (n - 1):
        return lax.div(x, jnp.int32(n)), lax.rem(x, jnp.int32(n))
    return lax.shift_right_logical(x, jnp.int32(n.bit_length() - 1)), x & jnp.int32(n - 1)


def fill_mix(filters_ref, pairs_ref, mix_ref, half):
    sources, stations, lags = filters_ref.shape
    points = mix_ref.shape[0] // sources
    snaps = points // half
    depth = mix_ref.shape[1]
    side = depth // 2
    shape = (snaps, stations * snaps)
    station, at = over(iota(shape, 1), snaps)
    lag = iota(shape, 0) - at + lags // 2
    same = over(iota((points, side), 0), half)[1] == over(iota((points, side), 1), half)[1]
    fans = [(over(iota((side, side), 1) + k * side, half)[0] == iota((side, side), 0)).astype(BF16) for k in range(2)]

    def spread(*accs):
        for unit in range(2):
            pltpu.matmul_push_rhs(fans[unit], staging_register=0, mxu_index=unit)
        for e in range(sources):
            table = jnp.zeros(shape, F32)
            for r in range(stations):
                used = pairs_ref[e, r].astype(F32)
                for j in range(lags):
                    table = jnp.where((station == r) & (lag == j), used * filters_ref[e, r, j], table)
            high = table.astype(BF16).astype(F32)
            taps = jnp.concatenate([high, table - high], axis=1)
            tall = jnp.broadcast_to(taps[:, None, :], (snaps, half, taps.shape[1])).reshape(points, taps.shape[1])
            lhs = jnp.concatenate([tall, jnp.zeros((points, side - taps.shape[1]), F32)], axis=1).astype(BF16)
            for unit in range(2):
                pltpu.matmul_acc_lhs(accs[unit], lhs, load_staged_rhs=0 if e == 0 else None)
                full = pltpu.matmul_pop(accs[unit])
                mix_ref[pl.ds(e * points, points), pl.ds(unit * side, side)] = jnp.where(same, full, 0.0).astype(BF16)

    pl.run_scoped(spread, *[pltpu.ACC(unit)((points, side), F32) for unit in range(2)])


def own_columns(displacement, me, slab, width, sizes):
    _, snaps, comps, planes, rows, _ = displacement.shape
    pieces = len(sizes)
    marks = [divmod(sum(sizes[:k]), snaps) for k in range(pieces)]

    def kernel(me_ref, slab_ref, src, *rest):
        outs, sems = rest[:-1], rest[-1]
        here = pl.ds(pl.multiple_of(me_ref[0] * width, width), width)
        copies = [
            pltpu.make_async_copy(src.at[e, pl.ds(s, size), :, :, :, here], outs[k], sems.at[k])
            for k, ((e, s), size) in enumerate(zip(marks, sizes))
        ]
        for copy in copies:
            copy.start()
        for copy in copies:
            copy.wait()

    return pl.pallas_call(
        kernel,
        out_shape=[jax.ShapeDtypeStruct((size, comps, planes, rows, width), displacement.dtype) for size in sizes],
        in_specs=[SMEM] * 2 + [ANY],
        out_specs=[VMEM] * pieces,
        scratch_shapes=[pltpu.SemaphoreType.DMA((pieces,))],
        compiler_params=pltpu.CompilerParams(vmem_limit_bytes=8 * 2**20),
        name="own_columns",
    )(me, slab, in_hbm(displacement))


def local_body(me, bits, first, tables, green_ref, added, z_ref, gs, xs, ys):
    mix_ref, dcol_ref, drow_ref, u_ref, lam_ref, mu_ref = tables
    count, _, planes, rows, width = z_ref.shape
    stations, snaps = green_ref.shape[:2]
    cols = u_ref.shape[-1]
    half = rows // 2
    points = snaps * half
    block = me ^ bits
    inside_half = pl.ds(pl.multiple_of((block & 1) * width, width), width)
    here = pl.ds(pl.multiple_of(block * width, width), width)
    before = pl.ds(pl.multiple_of(jnp.maximum(block * width - LANES, 0), LANES), LANES)
    behind = pl.ds(pl.multiple_of(jnp.minimum(block * width + width, cols - LANES), LANES), LANES)
    span = lambda h: pl.ds(h * half, half)
    space = lambda unit, size: pltpu.ACC(unit)((size, width), F32)

    lane = iota((half, LANES), 1)
    inner_left = jnp.where(block == 0, 0.0, 1.0)
    inner_right = jnp.where(block == cols // width - 1, 0.0, 1.0)
    left_2 = jnp.where(lane < 2, 1.0, 0.0) * inner_left
    left_1 = jnp.where(lane == 0, -8.0, 0.0) * inner_left
    right_2 = jnp.where(lane >= LANES - 2, -1.0, 0.0) * inner_right
    right_1 = jnp.where(lane == LANES - 1, 8.0, 0.0) * inner_right

    def one(index, carry):
        now, e = over(index, count)
        quake = first + e

        def filtered(h):
            def run(*accs):
                for k in range(3):
                    for unit in range(2):
                        tile = green_ref[:, :, 2 * k + unit, now, span(h), inside_half].reshape(stations * points, width)
                        pltpu.matmul_push_rhs(tile, staging_register=k % 2, mxu_index=unit)
                    for part in range(2):
                        row = pl.ds(pl.multiple_of(quake * points, points), points)
                        lhs = mix_ref[row, pl.ds(part * stations * points, stations * points)]
                        for unit in range(2):
                            acc = accs[2 * unit + k % 2]
                            pltpu.matmul_acc_lhs(acc, lhs, load_staged_rhs=k % 2 if part == 0 else None)
                    for unit in range(2):
                        gs[2 * k + unit, h] = pltpu.matmul_pop(accs[2 * unit + k % 2])

            pl.run_scoped(run, *[space(unit, points) for unit in range(2) for _ in range(2)])

        whole = [u_ref[quake, :, i, now, :, here].reshape(2 * points, width) for i in range(3)]

        def columns(*accs):
            for unit in range(2):
                pltpu.matmul_push_rhs(dcol_ref[...], staging_register=0, mxu_index=unit)
            for unit in range(2):
                pltpu.matmul_acc_lhs(accs[2 * unit], whole[unit], load_staged_rhs=0)
                pltpu.matmul_acc_lhs(accs[2 * unit + 1], whole[2][unit * points : (unit + 1) * points])
            for unit in range(2):
                xs[unit] = pltpu.matmul_pop(accs[2 * unit])
                xs[2, pl.ds(unit * points, points)] = pltpu.matmul_pop(accs[2 * unit + 1])

        def lines(*accs):
            for unit in range(2):
                pltpu.matmul_push_rhs(whole[unit], staging_register=0, mxu_index=unit)
                pltpu.matmul_push_rhs(whole[2], staging_register=1, mxu_index=unit)
            for unit in range(2):
                pltpu.matmul_acc_lhs(accs[3 * unit], drow_ref[0], load_staged_rhs=0)
                pltpu.matmul_acc_lhs(accs[3 * unit + 1], drow_ref[1])
                pltpu.matmul_acc_lhs(accs[3 * unit + 2], drow_ref[unit], load_staged_rhs=1)
            for unit in range(2):
                ys[unit, 0] = pltpu.matmul_pop(accs[3 * unit])
                ys[unit, 1] = pltpu.matmul_pop(accs[3 * unit + 1])
                ys[2, unit] = pltpu.matmul_pop(accs[3 * unit + 2])

        def along_columns(i, s, h):
            left = u_ref[quake, s, i, now, span(h), before].astype(F32)
            right = u_ref[quake, s, i, now, span(h), behind].astype(F32)
            left = pltpu.roll(left, 2, 1) * left_2 + pltpu.roll(left, 1, 1) * left_1
            right = pltpu.roll(right, LANES - 2, 1) * right_2 + pltpu.roll(right, LANES - 1, 1) * right_1
            inside = xs[i, pl.ds((2 * s + h) * half, half)]
            middle = inside[:, LANES : width - LANES]
            parts = [inside[:, :LANES] + left] + ([middle] if middle.shape[1] else [])
            return jnp.concatenate(parts + [inside[:, width - LANES :] + right], axis=1)

        def combine(h):
            vol = dev = jnp.zeros((half, width), F32)
            lam = lam_ref[now, span(h), here]
            mu2 = 2.0 * mu_ref[now, span(h), here]
            for s in range(snaps):
                at = pl.ds(s * half, half)
                xs0, xs1, xs2 = (along_columns(i, s, h) for i in range(3))
                gxx, gyy, gzz, gyz, gxz, gxy = (gs[c, h, at] for c in range(6))
                gtr = gxx + gyy + gzz
                dxx, dyy = xs0, ys[1, h, at]
                vol = vol + (dxx + dyy) * gtr
                dev = dev + (dxx * gxx + dyy * gyy) + (ys[2, h, at] * gyz + xs2 * gxz)
                dev = dev + (xs1 + ys[0, h, at]) * gxy
                for i, z in enumerate((mu2 * gxz, mu2 * gyz, lam * gtr + mu2 * gzz)):
                    for ref in added:
                        z = z + ref[e, i * snaps + s, now, span(h)].astype(F32)
                    z_ref[e, i * snaps + s, now, span(h)] = z.astype(BF16)
            part = (lam * vol + mu2 * dev) / 12.0
            for ref in added:
                part = part + two_parts(ref[e, 3 * snaps, now, span(h)], ref[e, 3 * snaps + 1, now, span(h)])
            high = part.astype(BF16)
            z_ref[e, 3 * snaps, now, span(h)] = high
            z_ref[e, 3 * snaps + 1, now, span(h)] = (part - high.astype(F32)).astype(BF16)

        pl.run_scoped(columns, *[space(unit, size) for unit in range(2) for size in (2 * points, points)])
        pl.run_scoped(lines, *[space(unit, points) for unit in range(2) for _ in range(3)])
        filtered(0)
        filtered(1)
        combine(0)
        combine(1)
        return carry

    lax.fori_loop(0, planes * count, one, 0)


def half_columns(ref, half, width):
    return ref.at[..., pl.ds(pl.multiple_of(half * 2 * width, 2 * width), 2 * width)]


def first_kernel(me_ref, filters_ref, pairs_ref, u_src, green_src, *rest, bits, waits):
    (lam_src, mu_src, dcol_src, drow_src), rest = rest[:4], rest[4 + waits :]
    z_ref, green_ref, mix_ref, dcol_ref, drow_ref, u_ref, lam_ref, mu_ref, gs, xs, ys, sems = rest
    rows, width = z_ref.shape[-2:]
    me = me_ref[0]
    block = me ^ bits

    def green_block(block, sem):
        there = pl.ds(pl.multiple_of(block * width, width), width)
        inside = pl.ds(pl.multiple_of((block & 1) * width, width), width)
        return pltpu.make_async_copy(green_src.at[..., there], green_ref.at[..., inside], sem)

    early = [pltpu.make_async_copy(u_src.at[0], u_ref.at[0], sems.at[6]), green_block(block, sems.at[0])]
    smalls = ((lam_src, lam_ref), (mu_src, mu_ref), (dcol_src, dcol_ref), (drow_src, drow_ref))
    early += [pltpu.make_async_copy(src, ref, sems.at[1 + k]) for k, (src, ref) in enumerate(smalls)]
    late = [green_block(block ^ 1, sems.at[5])]
    for copy in early:
        copy.start()
    fill_mix(filters_ref, pairs_ref, mix_ref, rows // 2)
    for copy in early:
        copy.wait()
    for copy in late:
        copy.start()
    local_body(me, bits, 0, (mix_ref, dcol_ref, drow_ref, u_ref, lam_ref, mu_ref), green_ref, (), z_ref, gs, xs, ys)
    for copy in late:
        copy.wait()


def z_shape(count, displacement, width):
    snaps, planes, rows = displacement.shape[1], displacement.shape[3], displacement.shape[4]
    return jax.ShapeDtypeStruct((count, 3 * snaps + 2, planes, rows, width), BF16)


def local_scratch(displacement, width):
    points = displacement.shape[1] * displacement.shape[4]
    return [
        pltpu.VMEM((6, 2, points // 2, width), F32),
        pltpu.VMEM((3, points, width), F32),
        pltpu.VMEM((3, 2, points // 2, width), F32),
    ]


def local_cost(count, green, displacement, width):
    _, snaps, _, planes, rows, _ = displacement.shape
    stations = green.shape[0]
    points = snaps * rows
    return pl.CostEstimate(
        flops=int(count * planes * 2 * width * points * (6 * stations * points + 3 * width + 3 * points)),
        bytes_accessed=int(count * planes * width * rows * snaps * (6 * stations + 9) * 2),
        transcendentals=0,
    )


def first_terms(me, bits, filters, pairs, displacement, green, lam, mu, width, after):
    sources, snaps, _, planes, rows, _ = displacement.shape
    stations = green.shape[0]
    fixed = stencils(snaps, rows, width)
    kept = [((stations, snaps, 6, planes, rows, 2 * width), green.dtype)]
    points = snaps * rows // 2
    kept.append(((sources * points, 2 * stations * points), BF16))
    kept += [(array.shape, array.dtype) for array in fixed + (displacement, lam, mu)]
    z, near, *tables = pl.pallas_call(
        functools.partial(first_kernel, bits=bits, waits=len(after)),
        out_shape=[z_shape(1, displacement, width)] + [pltpu.VMEM(*one) for one in kept],
        in_specs=[SMEM] * 3 + [ANY] * (6 + len(after)),
        out_specs=[VMEM] * (1 + len(kept)),
        scratch_shapes=local_scratch(displacement, width) + [pltpu.SemaphoreType.DMA((7,))],
        cost_estimate=local_cost(1, green, displacement, width),
        compiler_params=pltpu.CompilerParams(vmem_limit_bytes=16 * 2**20),
        name="first_terms",
    )(me, *map(in_hbm, (filters, pairs, displacement, green, lam, mu) + fixed), *after)
    return z, near, tuple(tables)


def local_kernel(me_ref, *refs, bits, first, waits, more, fetch, fill):
    me = me_ref[0]
    tables, green_ref, rest = refs[:6], refs[6], refs[7:]
    if fetch or fill:
        source, rest = rest[0], rest[1:]
    rest = rest[waits:]
    added, rest = rest[:more], rest[more:]
    if fetch:
        z_ref, other_ref, gs, xs, ys, sem = rest
        half = lax.shift_right_logical(me, 1)
        copy = pltpu.make_async_copy(half_columns(source, half, z_ref.shape[-1]), other_ref, sem)
        copy.start()
    elif fill:
        z_ref, u_ref, gs, xs, ys, sem = rest
        others = pl.ds(1, u_ref.shape[0] - 1)
        copy = pltpu.make_async_copy(source.at[others], u_ref.at[others], sem)
        copy.start()
    else:
        z_ref, gs, xs, ys = rest
    local_body(me, bits, first, tables, green_ref, added, z_ref, gs, xs, ys)
    if fetch or fill:
        copy.wait()


def local_terms(me, bits, first, count, tables, green_half, green, displacement, width, after=(), add=(), fetch=False, fill=False):
    out_shape = [z_shape(count, displacement, width)]
    scratch = local_scratch(displacement, width)
    if fetch:
        out_shape.append(pltpu.VMEM(green_half.shape, green_half.dtype))
        scratch.append(pltpu.SemaphoreType.DMA(()))
    if fill:
        out_shape.append(pltpu.VMEM(displacement.shape, displacement.dtype))
        scratch.append(pltpu.SemaphoreType.DMA(()))
    return pl.pallas_call(
        functools.partial(local_kernel, bits=bits, first=first, waits=len(after), more=len(add), fetch=fetch, fill=fill),
        out_shape=out_shape,
        in_specs=[SMEM] + [VMEM] * 7 + [ANY] * (fetch + fill + len(after)) + [VMEM] * len(add),
        out_specs=[VMEM] * len(out_shape),
        scratch_shapes=scratch,
        input_output_aliases={4: 1} if fill else {},
        cost_estimate=local_cost(count, green, displacement, width),
        compiler_params=pltpu.CompilerParams(vmem_limit_bytes=16 * 2**20),
        name="local_terms",
    )(me, *tables, green_half, *([in_hbm(green)] if fetch else [in_hbm(displacement)] if fill else []), *after, *map(in_vmem, add))


def depth_kernel(me_ref, slab_ref, *refs, groups, slabs, lasts):
    pieces, rest = refs[:lasts[0]], refs[lasts[0] :]
    z0_ref, z1_ref, outs = rest[0], rest[1], rest[2:]
    _, rows, width = z1_ref.shape[2:]
    source = lasts[1]
    snaps = (z1_ref.shape[1] - 2) // 3
    slab = slab_ref[0]
    even = slab % 2 == 0
    known = jnp.where(even, slab > 0, slab < slabs - 1).astype(F32)
    pick = lambda one, other: jnp.where(even, jnp.float32(one), jnp.float32(other))
    coefs = [pick(*both) for both in ((-1, 1), (0, -8), (1, -1), (-8, 0), (8, 0), (-1, 1), (0, 8), (1, -1))]
    coefs = [coef * known if k % 4 >= 2 else coef for k, coef in enumerate(coefs)]
    total = [
        sum(two_parts(ref[k, 3 * snaps, p], ref[k, 3 * snaps + 1, p]) for ref, k in ((z0_ref, source), (z1_ref, 0)))
        for p in range(2)
    ]
    carry = tuple(jnp.zeros((rows, width), F32) for _ in range(2))
    at = 0
    for own_ref, near_ref, far_ref in zip(pieces[0::3], pieces[1::3], pieces[2::3]):

        def step(s, carry, at=at, own_ref=own_ref, near_ref=near_ref, far_ref=far_ref):
            top, bottom = carry
            for i in range(3):
                own0, own1 = own_ref[s, i, 0].astype(F32), own_ref[s, i, 1].astype(F32)
                n0, n1 = near_ref[s, i, 0].astype(F32), near_ref[s, i, 1].astype(F32)
                f0, f1 = far_ref[s, i, 0].astype(F32), far_ref[s, i, 1].astype(F32)
                d0 = 8.0 * own1 + (coefs[0] * n0 + coefs[1] * n1) + (coefs[2] * f0 + coefs[3] * f1)
                d1 = (coefs[4] * n0 + coefs[5] * n1) + (coefs[6] * f0 + coefs[7] * f1) - 8.0 * own0
                k = i * snaps + at + s
                z = [z0_ref[source, k, p].astype(F32) + z1_ref[0, k, p].astype(F32) for p in range(2)]
                top = top + z[0] * d0
                bottom = bottom + z[1] * d1
            return top, bottom

        count = own_ref.shape[0]
        carry = lax.fori_loop(0, count, step, carry, unroll=2)
        at += count
    part = rows // groups
    held = outs[-1]
    for p in range(2):
        value = total[p] + carry[p] / 12.0
        for q in range(groups):
            held[q, p] = value[q * part : (q + 1) * part]
    for bits, out in enumerate(outs[:-1]):
        out[...] = held[me_ref[0] ^ bits]


def depth_terms(me, slab, pieces, z0, z1, source, groups, slabs):
    planes, rows, width = z1.shape[2:]
    shape = (planes, rows // groups, width)
    flat = [array for piece in pieces for array in piece]
    return pl.pallas_call(
        functools.partial(depth_kernel, groups=groups, slabs=slabs, lasts=(len(flat), source)),
        out_shape=[jax.ShapeDtypeStruct(shape, F32)] * groups,
        in_specs=[SMEM, SMEM] + [VMEM] * (len(flat) + 2),
        out_specs=[VMEM] * groups,
        scratch_shapes=[pltpu.VMEM((groups,) + shape, F32)],
        compiler_params=pltpu.CompilerParams(vmem_limit_bytes=8 * 2**20),
        name="depth_terms",
    )(me, slab, *map(in_vmem, flat + [z0, z1]))


def join_kernel(me_ref, *refs):
    pieces, out = refs[:-1], refs[-1]
    sources = out.shape[0]
    width = pieces[0].shape[-1]
    for k, piece in enumerate(pieces):
        bits, e = divmod(k, sources)
        out[e, :, :, pl.ds(pl.multiple_of((me_ref[0] ^ bits) * width, width), width)] = piece[...]


def join_columns(me, pieces, sources):
    planes, part, width = pieces[0].shape
    return pl.pallas_call(
        join_kernel,
        out_shape=jax.ShapeDtypeStruct((sources, planes, part, width * len(pieces) // sources), F32),
        in_specs=[SMEM] + [VMEM] * len(pieces),
        out_specs=VMEM,
        compiler_params=pltpu.CompilerParams(vmem_limit_bytes=8 * 2**20),
        name="join_columns",
    )(me, *map(in_vmem, pieces))


SHARES = (4, 4, 5, 3)


def on_device(displacement, green, lame_lambda, shear_modulus, filters, pairs):
    sources, snaps, _, _, _, cols = displacement.shape
    groups = lax.axis_size("rcv")
    slabs = lax.axis_size("slab")
    me = lax.axis_index("rcv").reshape(1)
    slab = lax.axis_index("slab").reshape(1)
    width = cols // groups
    pair_swap = [(i, i ^ 1) for i in range(slabs)]
    back = [(i, i - 2 if i % 2 == 0 else i + 2) for i in range(slabs)]
    back = [(i, j) for i, j in back if 0 <= j < slabs]
    chain = [(i, i + 2 if i % 2 == 0 else i - 2) for i in range(slabs)]
    chain = [(i, j) for i, j in chain if 0 <= j < slabs]
    onward = [(i, (i + 2 if i % 2 == 0 else i - 2) % slabs) for i in range(slabs)]

    def swap(x, bit):
        return lax.ppermute(x, "rcv", [(i, i ^ bit) for i in range(groups)])

    def along(x, links):
        return lax.ppermute(x, "slab", links)

    def terms(bits, first, count, half, after=(), add=(), **extra):
        return local_terms(me, bits, first, count, tables, half, green, displacement, width, after, add, **extra)

    total_snaps = sources * snaps
    unit = total_snaps // sum(SHARES)
    sizes = [share * unit for share in SHARES]
    own = own_columns(displacement, me, slab, width, sizes)
    near = [along(piece, pair_swap) for piece in own]
    far = [along(piece, onward if k < len(near) - 2 else chain) for k, piece in enumerate(near[:-1])]
    last = len(own) - 1
    far.append(along(along(own[last], back), pair_swap))

    across = []
    for e in range(sources):
        if e == 0:
            last, far_half, tables = first_terms(
                me, 3, filters, pairs, displacement, green, lame_lambda, shear_modulus, width, (own[0],)
            )
        else:
            last, near_half = terms(3, e, 1, far_half, (last,), fetch=True)
        sent = swap(last, 1)
        last, *filled = terms(2, e, 1, far_half, (last,), (sent,), fill=e == 0)
        if filled:
            tables = tables[:3] + tuple(filled) + tables[4:]
        across.append(swap(last, 2))
    (last,) = terms(1, 0, sources, near_half, (last,))
    (z0,) = terms(0, 0, sources, near_half, (last,), (swap(last, 1),))

    pieces = []
    for e in range(sources):
        mine = [k for k in range(len(SHARES)) if sum(sizes[:k]) // snaps == e]
        pieces.append(depth_terms(me, slab, [(own[k], near[k], far[k]) for k in mine], z0, across[e], e, groups, slabs))
    ends = []
    for bits in range(groups):
        for e in range(sources):
            piece = pieces[e][bits]
            ends.append(swap(piece, bits) if bits else piece)
    return join_columns(me, ends, sources)


def solution(mesh):
    placed = (
        P(None, None, None, "slab", None, None),
        P("rcv", None, None, "slab", None, None),
        P("slab", None, None),
        P("slab", None, None),
        P(None, "rcv", None),
        P(None, "rcv"),
    )
    return jax.shard_map(
        on_device,
        mesh=mesh,
        in_specs=placed,
        out_specs=P(None, "slab", "rcv", None),
        check_vma=False,
    )
```

```python
import functools
import jax
import jax.numpy as jnp
import numpy as np
from jax import lax
from jax.experimental import pallas as pl
from jax.experimental.pallas import tpu as pltpu
from jax.sharding import PartitionSpec as P

LANES = 128
F32 = jnp.float32
BF16 = jnp.bfloat16
ANY = pl.BlockSpec(memory_space=pl.ANY)
SMEM = pl.BlockSpec(memory_space=pltpu.SMEM)
VMEM = pl.BlockSpec(memory_space=pltpu.VMEM)


def stencil(offset):
    return 8.0 * (offset == 1) - 8.0 * (offset == -1) - 1.0 * (offset == 2) + 1.0 * (offset == -2)


def stencils(snaps, rows, width):
    place = np.arange(width)
    dcol = stencil(place[:, None] - place[None, :])
    snap = np.arange(snaps)
    same = snap[:, None] == snap[None, :]
    drow = []
    for h in range(2):
        row = np.arange(rows // 2) + h * (rows // 2)
        band = stencil(np.arange(rows)[None, :] - row[:, None])
        drow.append(np.kron(same, band))
    return jnp.asarray(dcol, BF16), jnp.asarray(np.stack(drow), BF16)


def iota(shape, axis):
    return lax.broadcasted_iota(jnp.int32, shape, axis)


def in_vmem(x):
    return pltpu.with_memory_space_constraint(x, pltpu.VMEM)


def in_hbm(x):
    return pltpu.with_memory_space_constraint(x, pltpu.HBM)


def two_parts(high, low):
    return high.astype(F32) + low.astype(F32)


def over(x, n):
    if n & (n - 1):
        return lax.div(x, jnp.int32(n)), lax.rem(x, jnp.int32(n))
    return lax.shift_right_logical(x, jnp.int32(n.bit_length() - 1)), x & jnp.int32(n - 1)


def fill_mix(filters_ref, pairs_ref, mix_ref, half):
    sources, stations, lags = filters_ref.shape
    points = mix_ref.shape[0] // sources
    snaps = points // half
    depth = mix_ref.shape[1]
    side = depth // 2
    shape = (snaps, stations * snaps)
    station, at = over(iota(shape, 1), snaps)
    lag = iota(shape, 0) - at + lags // 2
    same = over(iota((points, side), 0), half)[1] == over(iota((points, side), 1), half)[1]
    fans = [(over(iota((side, side), 1) + k * side, half)[0] == iota((side, side), 0)).astype(BF16) for k in range(2)]

    def spread(*accs):
        for unit in range(2):
            pltpu.matmul_push_rhs(fans[unit], staging_register=0, mxu_index=unit)
        for e in range(sources):
            table = jnp.zeros(shape, F32)
            for r in range(stations):
                used = pairs_ref[e, r].astype(F32)
                for j in range(lags):
                    table = jnp.where((station == r) & (lag == j), used * filters_ref[e, r, j], table)
            high = table.astype(BF16).astype(F32)
            taps = jnp.concatenate([high, table - high], axis=1)
            tall = jnp.broadcast_to(taps[:, None, :], (snaps, half, taps.shape[1])).reshape(points, taps.shape[1])
            lhs = jnp.concatenate([tall, jnp.zeros((points, side - taps.shape[1]), F32)], axis=1).astype(BF16)
            for unit in range(2):
                pltpu.matmul_acc_lhs(accs[unit], lhs, load_staged_rhs=0 if e == 0 else None)
                full = pltpu.matmul_pop(accs[unit])
                mix_ref[pl.ds(e * points, points), pl.ds(unit * side, side)] = jnp.where(same, full, 0.0).astype(BF16)

    pl.run_scoped(spread, *[pltpu.ACC(unit)((points, side), F32) for unit in range(2)])


def own_columns(displacement, me, slab, width, sizes):
    _, snaps, comps, planes, rows, _ = displacement.shape
    pieces = len(sizes)
    marks = [divmod(sum(sizes[:k]), snaps) for k in range(pieces)]

    def kernel(me_ref, slab_ref, src, *rest):
        outs, sems = rest[:-1], rest[-1]
        here = pl.ds(pl.multiple_of(me_ref[0] * width, width), width)
        copies = [
            pltpu.make_async_copy(src.at[e, pl.ds(s, size), :, :, :, here], outs[k], sems.at[k])
            for k, ((e, s), size) in enumerate(zip(marks, sizes))
        ]
        for copy in copies:
            copy.start()
        for copy in copies:
            copy.wait()

    return pl.pallas_call(
        kernel,
        out_shape=[jax.ShapeDtypeStruct((size, comps, planes, rows, width), displacement.dtype) for size in sizes],
        in_specs=[SMEM] * 2 + [ANY],
        out_specs=[VMEM] * pieces,
        scratch_shapes=[pltpu.SemaphoreType.DMA((pieces,))],
        compiler_params=pltpu.CompilerParams(vmem_limit_bytes=8 * 2**20),
        name="own_columns",
    )(me, slab, in_hbm(displacement))


def local_body(me, bits, first, tables, green_ref, added, z_ref, gs, xs, ys):
    mix_ref, dcol_ref, drow_ref, u_ref, lam_ref, mu_ref = tables
    count, _, planes, rows, width = z_ref.shape
    stations, snaps = green_ref.shape[:2]
    cols = u_ref.shape[-1]
    half = rows // 2
    points = snaps * half
    block = me ^ bits
    inside_half = pl.ds(pl.multiple_of((block & 1) * width, width), width)
    here = pl.ds(pl.multiple_of(block * width, width), width)
    before = pl.ds(pl.multiple_of(jnp.maximum(block * width - LANES, 0), LANES), LANES)
    behind = pl.ds(pl.multiple_of(jnp.minimum(block * width + width, cols - LANES), LANES), LANES)
    span = lambda h: pl.ds(h * half, half)
    space = lambda unit, size: pltpu.ACC(unit)((size, width), F32)

    lane = iota((half, LANES), 1)
    inner_left = jnp.where(block == 0, 0.0, 1.0)
    inner_right = jnp.where(block == cols // width - 1, 0.0, 1.0)
    left_2 = jnp.where(lane < 2, 1.0, 0.0) * inner_left
    left_1 = jnp.where(lane == 0, -8.0, 0.0) * inner_left
    right_2 = jnp.where(lane >= LANES - 2, -1.0, 0.0) * inner_right
    right_1 = jnp.where(lane == LANES - 1, 8.0, 0.0) * inner_right

    def one(index, carry):
        now, e = over(index, count)
        quake = first + e

        def filtered(h):
            def run(*accs):
                for k in range(3):
                    for unit in range(2):
                        tile = green_ref[:, :, 2 * k + unit, now, span(h), inside_half].reshape(stations * points, width)
                        pltpu.matmul_push_rhs(tile, staging_register=k % 2, mxu_index=unit)
                    for part in range(2):
                        row = pl.ds(pl.multiple_of(quake * points, points), points)
                        lhs = mix_ref[row, pl.ds(part * stations * points, stations * points)]
                        for unit in range(2):
                            acc = accs[2 * unit + k % 2]
                            pltpu.matmul_acc_lhs(acc, lhs, load_staged_rhs=k % 2 if part == 0 else None)
                    for unit in range(2):
                        gs[2 * k + unit, h] = pltpu.matmul_pop(accs[2 * unit + k % 2])

            pl.run_scoped(run, *[space(unit, points) for unit in range(2) for _ in range(2)])

        whole = [u_ref[quake, :, i, now, :, here].reshape(2 * points, width) for i in range(3)]

        def columns(*accs):
            for unit in range(2):
                pltpu.matmul_push_rhs(dcol_ref[...], staging_register=0, mxu_index=unit)
            for unit in range(2):
                pltpu.matmul_acc_lhs(accs[2 * unit], whole[unit], load_staged_rhs=0)
                pltpu.matmul_acc_lhs(accs[2 * unit + 1], whole[2][unit * points : (unit + 1) * points])
            for unit in range(2):
                xs[unit] = pltpu.matmul_pop(accs[2 * unit])
                xs[2, pl.ds(unit * points, points)] = pltpu.matmul_pop(accs[2 * unit + 1])

        def lines(*accs):
            for unit in range(2):
                pltpu.matmul_push_rhs(whole[unit], staging_register=0, mxu_index=unit)
                pltpu.matmul_push_rhs(whole[2], staging_register=1, mxu_index=unit)
            for unit in range(2):
                pltpu.matmul_acc_lhs(accs[3 * unit], drow_ref[0], load_staged_rhs=0)
                pltpu.matmul_acc_lhs(accs[3 * unit + 1], drow_ref[1])
                pltpu.matmul_acc_lhs(accs[3 * unit + 2], drow_ref[unit], load_staged_rhs=1)
            for unit in range(2):
                ys[unit, 0] = pltpu.matmul_pop(accs[3 * unit])
                ys[unit, 1] = pltpu.matmul_pop(accs[3 * unit + 1])
                ys[2, unit] = pltpu.matmul_pop(accs[3 * unit + 2])

        def along_columns(i, s, h):
            left = u_ref[quake, s, i, now, span(h), before].astype(F32)
            right = u_ref[quake, s, i, now, span(h), behind].astype(F32)
            left = pltpu.roll(left, 2, 1) * left_2 + pltpu.roll(left, 1, 1) * left_1
            right = pltpu.roll(right, LANES - 2, 1) * right_2 + pltpu.roll(right, LANES - 1, 1) * right_1
            inside = xs[i, pl.ds((2 * s + h) * half, half)]
            middle = inside[:, LANES : width - LANES]
            parts = [inside[:, :LANES] + left] + ([middle] if middle.shape[1] else [])
            return jnp.concatenate(parts + [inside[:, width - LANES :] + right], axis=1)

        def combine(h):
            vol = dev = jnp.zeros((half, width), F32)
            lam = lam_ref[now, span(h), here]
            mu2 = 2.0 * mu_ref[now, span(h), here]
            for s in range(snaps):
                at = pl.ds(s * half, half)
                xs0, xs1, xs2 = (along_columns(i, s, h) for i in range(3))
                gxx, gyy, gzz, gyz, gxz, gxy = (gs[c, h, at] for c in range(6))
                gtr = gxx + gyy + gzz
                dxx, dyy = xs0, ys[1, h, at]
                vol = vol + (dxx + dyy) * gtr
                dev = dev + (dxx * gxx + dyy * gyy) + (ys[2, h, at] * gyz + xs2 * gxz)
                dev = dev + (xs1 + ys[0, h, at]) * gxy
                for i, z in enumerate((mu2 * gxz, mu2 * gyz, lam * gtr + mu2 * gzz)):
                    for ref in added:
                        z = z + ref[e, i * snaps + s, now, span(h)].astype(F32)
                    z_ref[e, i * snaps + s, now, span(h)] = z.astype(BF16)
            part = (lam * vol + mu2 * dev) / 12.0
            for ref in added:
                part = part + two_parts(ref[e, 3 * snaps, now, span(h)], ref[e, 3 * snaps + 1, now, span(h)])
            high = part.astype(BF16)
            z_ref[e, 3 * snaps, now, span(h)] = high
            z_ref[e, 3 * snaps + 1, now, span(h)] = (part - high.astype(F32)).astype(BF16)

        pl.run_scoped(columns, *[space(unit, size) for unit in range(2) for size in (2 * points, points)])
        pl.run_scoped(lines, *[space(unit, points) for unit in range(2) for _ in range(3)])
        filtered(0)
        filtered(1)
        combine(0)
        combine(1)
        return carry

    lax.fori_loop(0, planes * count, one, 0)


def half_columns(ref, half, width):
    return ref.at[..., pl.ds(pl.multiple_of(half * 2 * width, 2 * width), 2 * width)]


def first_kernel(me_ref, filters_src, pairs_src, u_src, green_src, *rest, bits, waits):
    (lam_src, mu_src, dcol_src, drow_src), rest = rest[:4], rest[4 + waits :]
    z_ref, green_ref, mix_ref, dcol_ref, drow_ref, u_ref, lam_ref, mu_ref, gs, xs, ys, filters_ref, pairs_ref, sems = rest
    rows, width = z_ref.shape[-2:]
    me = me_ref[0]
    block = me ^ bits

    def green_block(block, sem):
        there = pl.ds(pl.multiple_of(block * width, width), width)
        inside = pl.ds(pl.multiple_of((block & 1) * width, width), width)
        return pltpu.make_async_copy(green_src.at[..., there], green_ref.at[..., inside], sem)

    early = [pltpu.make_async_copy(u_src.at[0], u_ref.at[0], sems.at[6]), green_block(block, sems.at[0])]
    smalls = ((lam_src, lam_ref), (mu_src, mu_ref), (dcol_src, dcol_ref), (drow_src, drow_ref))
    early += [pltpu.make_async_copy(src, ref, sems.at[1 + k]) for k, (src, ref) in enumerate(smalls)]
    late = [green_block(block ^ 1, sems.at[5])]
    for copy in early:
        copy.start()
    scalars = ((filters_src, filters_ref), (pairs_src, pairs_ref))
    scalars = [pltpu.make_async_copy(src, ref, sems.at[7 + k]) for k, (src, ref) in enumerate(scalars)]
    for copy in scalars:
        copy.start()
    for copy in scalars:
        copy.wait()
    fill_mix(filters_ref, pairs_ref, mix_ref, rows // 2)
    for copy in early:
        copy.wait()
    for copy in late:
        copy.start()
    local_body(me, bits, 0, (mix_ref, dcol_ref, drow_ref, u_ref, lam_ref, mu_ref), green_ref, (), z_ref, gs, xs, ys)
    for copy in late:
        copy.wait()


def z_shape(count, displacement, width):
    snaps, planes, rows = displacement.shape[1], displacement.shape[3], displacement.shape[4]
    return jax.ShapeDtypeStruct((count, 3 * snaps + 2, planes, rows, width), BF16)


def local_scratch(displacement, width):
    points = displacement.shape[1] * displacement.shape[4]
    return [
        pltpu.VMEM((6, 2, points // 2, width), F32),
        pltpu.VMEM((3, points, width), F32),
        pltpu.VMEM((3, 2, points // 2, width), F32),
    ]


def local_cost(count, green, displacement, width):
    _, snaps, _, planes, rows, _ = displacement.shape
    stations = green.shape[0]
    points = snaps * rows
    return pl.CostEstimate(
        flops=int(count * planes * 2 * width * points * (6 * stations * points + 3 * width + 3 * points)),
        bytes_accessed=int(count * planes * width * rows * snaps * (6 * stations + 9) * 2),
        transcendentals=0,
    )


def first_terms(me, bits, filters, pairs, displacement, green, lam, mu, width, after):
    sources, snaps, _, planes, rows, _ = displacement.shape
    stations = green.shape[0]
    fixed = stencils(snaps, rows, width)
    kept = [((stations, snaps, 6, planes, rows, 2 * width), green.dtype)]
    points = snaps * rows // 2
    kept.append(((sources * points, 2 * stations * points), BF16))
    kept += [(array.shape, array.dtype) for array in fixed + (displacement, lam, mu)]
    z, near, *tables = pl.pallas_call(
        functools.partial(first_kernel, bits=bits, waits=len(after)),
        out_shape=[z_shape(1, displacement, width)] + [pltpu.VMEM(*one) for one in kept],
        in_specs=[SMEM] + [ANY] * (8 + len(after)),
        out_specs=[VMEM] * (1 + len(kept)),
        scratch_shapes=local_scratch(displacement, width)
        + [pltpu.SMEM(array.shape, array.dtype) for array in (filters, pairs)]
        + [pltpu.SemaphoreType.DMA((9,))],
        cost_estimate=local_cost(1, green, displacement, width),
        compiler_params=pltpu.CompilerParams(vmem_limit_bytes=16 * 2**20),
        name="first_terms",
    )(me, *map(in_hbm, (filters, pairs, displacement, green, lam, mu) + fixed), *after)
    return z, near, tuple(tables)


def local_kernel(me_ref, *refs, bits, first, waits, more, fetch, fill):
    me = me_ref[0]
    tables, green_ref, rest = refs[:6], refs[6], refs[7:]
    if fetch or fill:
        source, rest = rest[0], rest[1:]
    rest = rest[waits:]
    added, rest = rest[:more], rest[more:]
    if fetch:
        z_ref, other_ref, gs, xs, ys, sem = rest
        half = lax.shift_right_logical(me, 1)
        copy = pltpu.make_async_copy(half_columns(source, half, z_ref.shape[-1]), other_ref, sem)
        copy.start()
    elif fill:
        z_ref, u_ref, gs, xs, ys, sem = rest
        others = pl.ds(1, u_ref.shape[0] - 1)
        copy = pltpu.make_async_copy(source.at[others], u_ref.at[others], sem)
        copy.start()
    else:
        z_ref, gs, xs, ys = rest
    local_body(me, bits, first, tables, green_ref, added, z_ref, gs, xs, ys)
    if fetch or fill:
        copy.wait()


def local_terms(me, bits, first, count, tables, green_half, green, displacement, width, after=(), add=(), fetch=False, fill=False):
    out_shape = [z_shape(count, displacement, width)]
    scratch = local_scratch(displacement, width)
    if fetch:
        out_shape.append(pltpu.VMEM(green_half.shape, green_half.dtype))
        scratch.append(pltpu.SemaphoreType.DMA(()))
    if fill:
        out_shape.append(pltpu.VMEM(displacement.shape, displacement.dtype))
        scratch.append(pltpu.SemaphoreType.DMA(()))
    return pl.pallas_call(
        functools.partial(local_kernel, bits=bits, first=first, waits=len(after), more=len(add), fetch=fetch, fill=fill),
        out_shape=out_shape,
        in_specs=[SMEM] + [VMEM] * 7 + [ANY] * (fetch + fill + len(after)) + [VMEM] * len(add),
        out_specs=[VMEM] * len(out_shape),
        scratch_shapes=scratch,
        input_output_aliases={4: 1} if fill else {},
        cost_estimate=local_cost(count, green, displacement, width),
        compiler_params=pltpu.CompilerParams(vmem_limit_bytes=16 * 2**20),
        name="local_terms",
    )(me, *tables, green_half, *([in_hbm(green)] if fetch else [in_hbm(displacement)] if fill else []), *after, *map(in_vmem, add))


def depth_kernel(me_ref, slab_ref, *refs, groups, slabs, lasts):
    pieces, rest = refs[:lasts[0]], refs[lasts[0] :]
    z0_ref, z1_ref, outs = rest[0], rest[1], rest[2:]
    _, rows, width = z1_ref.shape[2:]
    source = lasts[1]
    snaps = (z1_ref.shape[1] - 2) // 3
    slab = slab_ref[0]
    even = slab % 2 == 0
    known = jnp.where(even, slab > 0, slab < slabs - 1).astype(F32)
    pick = lambda one, other: jnp.where(even, jnp.float32(one), jnp.float32(other))
    coefs = [pick(*both) for both in ((-1, 1), (0, -8), (1, -1), (-8, 0), (8, 0), (-1, 1), (0, 8), (1, -1))]
    coefs = [coef * known if k % 4 >= 2 else coef for k, coef in enumerate(coefs)]
    total = [
        sum(two_parts(ref[k, 3 * snaps, p], ref[k, 3 * snaps + 1, p]) for ref, k in ((z0_ref, source), (z1_ref, 0)))
        for p in range(2)
    ]
    carry = tuple(jnp.zeros((rows, width), F32) for _ in range(2))
    at = 0
    for own_ref, near_ref, far_ref in zip(pieces[0::3], pieces[1::3], pieces[2::3]):

        def step(s, carry, at=at, own_ref=own_ref, near_ref=near_ref, far_ref=far_ref):
            top, bottom = carry
            for i in range(3):
                own0, own1 = own_ref[s, i, 0].astype(F32), own_ref[s, i, 1].astype(F32)
                n0, n1 = near_ref[s, i, 0].astype(F32), near_ref[s, i, 1].astype(F32)
                f0, f1 = far_ref[s, i, 0].astype(F32), far_ref[s, i, 1].astype(F32)
                d0 = 8.0 * own1 + (coefs[0] * n0 + coefs[1] * n1) + (coefs[2] * f0 + coefs[3] * f1)
                d1 = (coefs[4] * n0 + coefs[5] * n1) + (coefs[6] * f0 + coefs[7] * f1) - 8.0 * own0
                k = i * snaps + at + s
                z = [z0_ref[source, k, p].astype(F32) + z1_ref[0, k, p].astype(F32) for p in range(2)]
                top = top + z[0] * d0
                bottom = bottom + z[1] * d1
            return top, bottom

        count = own_ref.shape[0]
        carry = lax.fori_loop(0, count, step, carry, unroll=2)
        at += count
    part = rows // groups
    held = outs[-1]
    for p in range(2):
        value = total[p] + carry[p] / 12.0
        for q in range(groups):
            held[q, p] = value[q * part : (q + 1) * part]
    for bits, out in enumerate(outs[:-1]):
        out[...] = held[me_ref[0] ^ bits]


def depth_terms(me, slab, pieces, z0, z1, source, groups, slabs):
    planes, rows, width = z1.shape[2:]
    shape = (planes, rows // groups, width)
    flat = [array for piece in pieces for array in piece]
    return pl.pallas_call(
        functools.partial(depth_kernel, groups=groups, slabs=slabs, lasts=(len(flat), source)),
        out_shape=[jax.ShapeDtypeStruct(shape, F32)] * groups,
        in_specs=[SMEM, SMEM] + [VMEM] * (len(flat) + 2),
        out_specs=[VMEM] * groups,
        scratch_shapes=[pltpu.VMEM((groups,) + shape, F32)],
        compiler_params=pltpu.CompilerParams(vmem_limit_bytes=8 * 2**20),
        name="depth_terms",
    )(me, slab, *map(in_vmem, flat + [z0, z1]))


def join_kernel(me_ref, *refs):
    pieces, out = refs[:-1], refs[-1]
    sources = out.shape[0]
    width = pieces[0].shape[-1]
    for k, piece in enumerate(pieces):
        bits, e = divmod(k, sources)
        out[e, :, :, pl.ds(pl.multiple_of((me_ref[0] ^ bits) * width, width), width)] = piece[...]


def join_columns(me, pieces, sources):
    planes, part, width = pieces[0].shape
    return pl.pallas_call(
        join_kernel,
        out_shape=jax.ShapeDtypeStruct((sources, planes, part, width * len(pieces) // sources), F32),
        in_specs=[SMEM] + [VMEM] * len(pieces),
        out_specs=VMEM,
        compiler_params=pltpu.CompilerParams(vmem_limit_bytes=8 * 2**20),
        name="join_columns",
    )(me, *map(in_vmem, pieces))


SHARES = (4, 4, 5, 3)


def on_device(displacement, green, lame_lambda, shear_modulus, filters, pairs):
    sources, snaps, _, _, _, cols = displacement.shape
    groups = lax.axis_size("rcv")
    slabs = lax.axis_size("slab")
    me = lax.axis_index("rcv").reshape(1)
    slab = lax.axis_index("slab").reshape(1)
    width = cols // groups
    pair_swap = [(i, i ^ 1) for i in range(slabs)]
    back = [(i, i - 2 if i % 2 == 0 else i + 2) for i in range(slabs)]
    back = [(i, j) for i, j in back if 0 <= j < slabs]
    chain = [(i, i + 2 if i % 2 == 0 else i - 2) for i in range(slabs)]
    chain = [(i, j) for i, j in chain if 0 <= j < slabs]
    onward = [(i, (i + 2 if i % 2 == 0 else i - 2) % slabs) for i in range(slabs)]

    def swap(x, bit):
        return lax.ppermute(x, "rcv", [(i, i ^ bit) for i in range(groups)])

    def along(x, links):
        return lax.ppermute(x, "slab", links)

    def terms(bits, first, count, half, after=(), add=(), **extra):
        return local_terms(me, bits, first, count, tables, half, green, displacement, width, after, add, **extra)

    total_snaps = sources * snaps
    unit = total_snaps // sum(SHARES)
    sizes = [share * unit for share in SHARES]
    own = own_columns(displacement, me, slab, width, sizes)
    near = [along(piece, pair_swap) for piece in own]
    far = [along(piece, onward if k < len(near) - 2 else chain) for k, piece in enumerate(near[:-1])]
    last = len(own) - 1
    far.append(along(along(own[last], back), pair_swap))

    across = []
    for e in range(sources):
        if e == 0:
            last, far_half, tables = first_terms(
                me, 3, filters, pairs, displacement, green, lame_lambda, shear_modulus, width, (own[0],)
            )
        else:
            last, near_half = terms(3, e, 1, far_half, (last,), fetch=True)
        sent = swap(last, 1)
        last, *filled = terms(2, e, 1, far_half, (last,), (sent,), fill=e == 0)
        if filled:
            tables = tables[:3] + tuple(filled) + tables[4:]
        across.append(swap(last, 2))
    (last,) = terms(1, 0, sources, near_half, (last,))
    (z0,) = terms(0, 0, sources, near_half, (last,), (swap(last, 1),))

    pieces = []
    for e in range(sources):
        mine = [k for k in range(len(SHARES)) if sum(sizes[:k]) // snaps == e]
        pieces.append(depth_terms(me, slab, [(own[k], near[k], far[k]) for k in mine], z0, across[e], e, groups, slabs))
    ends = []
    for bits in range(groups):
        for e in range(sources):
            piece = pieces[e][bits]
            ends.append(swap(piece, bits) if bits else piece)
    return join_columns(me, ends, sources)


def solution(mesh):
    placed = (
        P(None, None, None, "slab", None, None),
        P("rcv", None, None, "slab", None, None),
        P("slab", None, None),
        P("slab", None, None),
        P(None, "rcv", None),
        P(None, "rcv"),
    )
    return jax.shard_map(
        on_device,
        mesh=mesh,
        in_specs=placed,
        out_specs=P(None, "slab", "rcv", None),
        check_vma=False,
    )
```
